32 devices in a mesh: rows: 8 (over z, y), rep: 4 (over x, core).
Axes of the slice: x: 2, y: 2, z: 4, core: 2. Of those that a mesh axis runs over, the one named last changes fastest.
Arguments:
- embed: bfloat16 [4096, 1024], P('rows'), may hold values from -6 to 6
- start: bfloat16 [4096, 128], P('rows'), may hold values from -6 to 6
- links: int32 [8, 8], P('rows'), may hold values from -1 to 3, as said below
Outputs:
- embedding: float32 [4096, 128], P('rows')
The draws below stay inside these ranges and needn't reach their ends.
Inputs may be any that keep to these rules, and one draw needn't show every extreme that they name: `links`: entry [r, s] is -1 (no pair) or a block of owner s; the diagonal is -1; each row has at most 6 entries other than -1, and some row has exactly 6.
All inputs are finite; a program needn't handle non-finite values.
Results may differ from the reference program's by a relative error of at most 0.012.
Values may be sent and summed in bfloat16 or wider, within the bound.
A program may use at most 128 MiB of HBM per device.

```python
import math
import jax
import jax.numpy as jnp
from jax import lax

D = 1024
K = 128
BLOCK = 128
BLOCKS_DEV = 4
ITERS = 2
POINTS = 4096
LINK_MAX = 6
N_ROWS = 8


def draw_links(key, part):
    base_key = jax.random.fold_in(key, 11)
    level_key, busy_key, order_key, block_key = jax.random.split(base_key, 4)
    owner_ids = jnp.arange(N_ROWS)
    levels = jax.random.randint(level_key, (N_ROWS,), 0, 2)
    counts = jnp.maximum(jnp.right_shift(jnp.full((N_ROWS,), LINK_MAX, jnp.int32), levels), 1)
    busiest = jax.random.randint(busy_key, (), 0, N_ROWS)
    counts = jnp.where(owner_ids == busiest, LINK_MAX, counts)
    row_keys = jax.random.split(order_key, N_ROWS)
    shuffles = jax.vmap(lambda row_key: jax.random.permutation(row_key, N_ROWS))(row_keys)
    rank_order = jnp.argsort(shuffles, axis=1, stable=True)
    self_rank = jnp.sum(jnp.where(owner_ids[:, None] == owner_ids[None, :], rank_order, 0), axis=1)
    other_rank = rank_order - (rank_order > self_rank[:, None]).astype(jnp.int32)
    is_self = owner_ids[:, None] == owner_ids[None, :]
    alive_link = jnp.logical_and(other_rank < counts[:, None], jnp.logical_not(is_self))
    chosen = jax.random.randint(block_key, (N_ROWS, N_ROWS), 0, BLOCKS_DEV)
    return jnp.where(alive_link, chosen, -1).astype(jnp.int32)


def block_scale(rng, shape, shards, low, top_value):
    def one(axis_at, shards_of):
        draws = jax.random.uniform(jax.random.fold_in(jax.random.fold_in(rng, 6), axis_at), (shards_of,), jnp.float32, low / len(shards), top_value / len(shards))
        return jnp.repeat(jnp.exp(draws), shape[axis_at] // shards_of).reshape((-1,) + (1,) * (len(shape) - axis_at - 1))

    loudness = one(*shards[0])
    for cut in shards[1:]:
        loudness = loudness * one(*cut)
    return loudness


def gaussian(rng, dims, width, bound, cuts=(), held_as=jnp.bfloat16):
    values = width * jax.random.normal(rng, dims, jnp.float32)
    if cuts:
        values = values * block_scale(rng, dims, cuts, -0.22, 0.18)
    return jnp.clip(values, -bound, bound).astype(held_as)


def setup_inputs(seed: int = 0) -> dict:
    keys = jax.random.split(jax.random.key(seed), 4)
    embed = gaussian(keys[0], (POINTS, D), 1.0, 6.0, ((0, 8),))
    start = gaussian(keys[1], (POINTS, K), 1.0, 6.0, ((0, 8),))
    links = draw_links(jax.random.fold_in(keys[3], 71), 0)
    return {"embed": embed, "start": start, "links": links}


EPSILON = 1e-06

def row_scale(rows):
    values = rows.astype(jnp.float32)
    return lax.rsqrt(lax.optimization_barrier(jnp.mean(values * values, axis=-1)) + EPSILON)

def orthonormal(result, gram_matrix):
    lower_factor = jnp.linalg.cholesky(gram_matrix)
    return lax.linalg.triangular_solve(lower_factor, result, left_side=False, lower=True, transpose_a=True)

def reference(embed, start, links):
    feature_count = embed.shape[1]
    comp_count = start.shape[1]
    spread = 2.0 / math.sqrt(feature_count)
    owners = links.shape[0]
    slab_rows = embed.shape[0] // owners
    blocks = slab_rows // BLOCK
    scales = row_scale(embed).reshape(owners, slab_rows)
    slabs = embed.reshape(owners, slab_rows, feature_count)
    block_rows = embed.reshape(owners, blocks, BLOCK, feature_count)
    block_scales = scales.reshape(owners, blocks, BLOCK)
    self_mask = jnp.arange(slab_rows)[:, None] == jnp.arange(slab_rows)[None, :]

    def owner_tiles(owner_index):
        link_row = lax.dynamic_index_in_dim(links, owner_index, 0, keepdims=False)
        slot_order = jnp.argsort((link_row < 0).astype(jnp.int32), stable=True)[:LINK_MAX].astype(jnp.int32)
        chosen = jnp.clip(link_row[slot_order], 0, blocks - 1).astype(jnp.int32)
        alive_slot = (link_row[slot_order] >= 0).astype(jnp.float32)
        pieces = block_rows[slot_order, chosen].reshape(-1, feature_count)
        piece_scale = block_scales[slot_order, chosen]
        own_rows = lax.dynamic_index_in_dim(slabs, owner_index, 0, keepdims=False)
        own_scale = lax.dynamic_index_in_dim(scales, owner_index, 0, keepdims=False)
        products_in = jnp.dot(pieces.astype(jnp.float32), own_rows.T.astype(jnp.float32), preferred_element_type=jnp.float32).reshape(LINK_MAX, BLOCK, slab_rows)
        exponent = spread * products_in * piece_scale[:, :, None] * own_scale[None, None, :]
        pair_tiles = (jnp.exp(exponent) * alive_slot[:, None, None]).astype(jnp.bfloat16)
        self_products = jnp.dot(own_rows.astype(jnp.float32), own_rows.T.astype(jnp.float32), preferred_element_type=jnp.float32)
        self_exponent = spread * self_products * own_scale[:, None] * own_scale[None, :]
        square = jnp.where(self_mask, 0.0, jnp.exp(self_exponent)).astype(jnp.bfloat16)
        return (slot_order, chosen, pair_tiles, square)

    def degree_step(summed_all, owner_index):
        slot_order, chosen, pair_tiles, square = owner_tiles(owner_index)
        own_sums = lax.optimization_barrier(jnp.sum(pair_tiles, axis=(0, 1), dtype=jnp.float32)) + lax.optimization_barrier(jnp.sum(square, axis=0, dtype=jnp.float32))
        back_sums = lax.optimization_barrier(jnp.sum(pair_tiles, axis=2, dtype=jnp.float32))
        summed_all = summed_all.at[owner_index].add(own_sums.reshape(blocks, BLOCK))
        summed_all = summed_all.at[slot_order, chosen].add(back_sums)
        return (summed_all, None)
    owner_ids = jnp.arange(owners, dtype=jnp.int32)
    degree = lax.scan(degree_step, jnp.zeros((owners, blocks, BLOCK), jnp.float32), owner_ids)[0].reshape(-1)
    inv_root = lax.rsqrt(degree)
    current = start.astype(jnp.float32)
    for turn_index in range(ITERS):
        scaled = (current * inv_root[:, None]).astype(jnp.bfloat16)
        scaled_slabs = scaled.reshape(owners, slab_rows, comp_count)
        scaled_blocks = scaled.reshape(owners, blocks, BLOCK, comp_count)

        def product_step(summed_all, owner_index):
            slot_order, chosen, pair_tiles, square = owner_tiles(owner_index)
            own_rows = lax.dynamic_index_in_dim(scaled_slabs, owner_index, 0, keepdims=False)
            fetched = scaled_blocks[slot_order, chosen].reshape(-1, comp_count)
            flat_rows = pair_tiles.reshape(-1, slab_rows)
            forward = jnp.dot(flat_rows.T.astype(jnp.float32), fetched.astype(jnp.float32), preferred_element_type=jnp.float32)
            forward = forward + jnp.dot(square.astype(jnp.float32), own_rows.astype(jnp.float32), preferred_element_type=jnp.float32)
            back_sums = jnp.dot(flat_rows.astype(jnp.float32), own_rows.astype(jnp.float32), preferred_element_type=jnp.float32).reshape(LINK_MAX, BLOCK, comp_count)
            summed_all = summed_all.at[owner_index].add(forward.reshape(blocks, BLOCK, comp_count))
            summed_all = summed_all.at[slot_order, chosen].add(back_sums)
            return (summed_all, None)
        zeros_all = jnp.zeros((owners, blocks, BLOCK, comp_count), jnp.float32)
        summed_all = lax.scan(product_step, zeros_all, owner_ids)[0].reshape(-1, comp_count)
        result = summed_all * inv_root[:, None]
        gram_matrix = jnp.dot(result.T, result, precision=lax.Precision.HIGHEST)
        current = orthonormal(result, gram_matrix)
    return current * math.sqrt(embed.shape[0])
```

```python
import functools
import math

import jax
import jax.numpy as jnp
from jax import lax
from jax.experimental import pallas as pl
from jax.experimental.pallas import tpu as pltpu
from jax.sharding import PartitionSpec as P

BLOCK = 128
BLOCKS_DEV = 4
ITERS = 2
LANES = 128
EPSILON = 1e-06
HIGHEST = lax.Precision.HIGHEST
F32 = jnp.float32
BF16 = jnp.bfloat16


def dot(a, b, dims, precision=None):
    return lax.dot_general(
        a, b, (dims, ((), ())), precision=precision, preferred_element_type=F32
    )


def inv_rms(rows):
    values = rows.astype(F32)
    return lax.rsqrt(jnp.mean(values * values, axis=1, keepdims=True) + EPSILON)


def as_row(column):
    return jnp.broadcast_to(column, (column.shape[0], LANES)).T[0:1, :]


def kernel(
    n, reps,
    embed, start, links, out,
    link_in, asked, alive, own, picks, pieces, tiles, tiles_t, square,
    u_full, u_out, u_in, rev_out, rev_in, part_out, part_in, y_own, y_in, inv, placed,
    g_out, g_in, slice_out, slice_in, total_out, gram, elim,
    link_send, link_recv, embed_send, embed_recv, u_send, u_recv, rev_send, rev_recv,
    part_send, part_recv, y_send, y_recv, g_send, g_recv, slice_send, slice_recv,
    total_send, total_recv,
):
    me = lax.axis_index("rows")
    quarter = lax.axis_index("rep")
    slab, features = embed.shape
    comps = start.shape[1]
    blocks = BLOCKS_DEV
    piece = BLOCK // reps
    own_rows = blocks * piece
    spread = 2.0 / math.sqrt(features)
    group = min(n, 8)
    chunk = group * piece
    unroll = n <= 8

    def over(count, body, low=0):
        if unroll:
            for index in range(low, count):
                body(index)
        else:
            def step(index, carry):
                body(index)
                return carry
            lax.fori_loop(low, count, step, 0)

    def peer(distance):
        return lax.rem(me + distance, n)

    def rep_peer(distance):
        return lax.rem(quarter + distance, reps)

    def to_rows(src, dst, send, recv, target):
        return pltpu.make_async_remote_copy(
            src_ref=src, dst_ref=dst, send_sem=send, recv_sem=recv,
            device_id={"rows": target}, device_id_type=pl.DeviceIdType.MESH,
        )

    def to_rep(src, dst, send, recv, target):
        return pltpu.make_async_remote_copy(
            src_ref=src, dst_ref=dst, send_sem=send, recv_sem=recv,
            device_id={"rep": target}, device_id_type=pl.DeviceIdType.MESH,
        )

    def own_at(block, which):
        return pl.ds(pl.multiple_of(block * BLOCK + which * piece, piece), piece)

    barrier = pltpu.get_barrier_semaphore()

    def greet(distance):
        pl.semaphore_signal(
            barrier, inc=1, device_id={"rows": peer(distance)},
            device_id_type=pl.DeviceIdType.MESH,
        )

    over(n, greet, 1)
    for distance in range(1, reps):
        pl.semaphore_signal(
            barrier, inc=1, device_id={"rep": rep_peer(distance)},
            device_id_type=pl.DeviceIdType.MESH,
        )
    pl.semaphore_wait(barrier, n + reps - 2)

    def link_copy(s):
        return to_rows(links, link_in.at[me], link_send.at[s], link_recv.at[me], s)

    def link_got(s):
        return to_rows(links, link_in.at[s], link_send.at[s], link_recv.at[s], s)

    over(n, lambda d: link_copy(peer(d)).start(), 1)
    lane = lax.broadcasted_iota(jnp.int32, (8, LANES), 1)
    link_in[me] = links[...]
    pieces[me] = jnp.zeros((piece, features), BF16)

    for b in range(blocks):
        own[b] = embed[own_at(b, quarter), :]
    own_flat = own[...].reshape(own_rows, features)
    own_scale = inv_rms(own_flat)
    slab_scale = jnp.concatenate(
        [inv_rms(embed[b * BLOCK:(b + 1) * BLOCK, :]) for b in range(blocks)], axis=0
    )
    scale_row = as_row(slab_scale)

    def alive_of(s):
        entry = jnp.sum(jnp.where(lane == s, links[...], 0).astype(F32), axis=1, keepdims=True)
        alive[s] = jnp.broadcast_to(
            jnp.where(entry[0:1] >= 0.0, 1.0, 0.0), (piece, LANES)
        )

    over(n, alive_of)

    def pick(d):
        s = peer(d)
        link_got(s).wait_recv()
        entry = jnp.sum(
            jnp.where(lane == me, link_in[s], 0).astype(F32), axis=1, keepdims=True
        )
        asked[s] = jnp.broadcast_to(entry, (8, LANES))
        chosen = jnp.maximum(entry[0:1], 0.0)
        mixed = jnp.zeros((piece, features), F32)
        for b in range(blocks):
            mixed = mixed + jnp.where(chosen == float(b), 1.0, 0.0) * own[b].astype(F32)
        picks[s] = mixed.astype(BF16)
        to_rows(picks.at[s], pieces.at[me], embed_send.at[s], embed_recv.at[me], s).start()

    over(n, pick, 1)

    products = dot(embed[...], own_flat, ((1,), (1,)))
    affinity = jnp.exp(spread * products * slab_scale * as_row(own_scale))
    row_id = lax.broadcasted_iota(jnp.int32, (slab, own_rows), 0)
    col_id = lax.broadcasted_iota(jnp.int32, (slab, own_rows), 1)
    col_row = (col_id // piece) * BLOCK + quarter * piece + col_id % piece
    square[...] = jnp.where(row_id == col_row, 0.0, affinity).astype(BF16)

    def embed_got(d):
        s = peer(d)
        to_rows(picks.at[s], pieces.at[s], embed_send.at[s], embed_recv.at[s], s).wait_recv()

    over(n, embed_got, 1)

    def tile_chunk(index):
        first = index * group
        rows = pieces[pl.ds(first, group)].reshape(chunk, features)
        live = alive[pl.ds(first, group)].reshape(chunk, LANES)[:, 0:1]
        values = dot(rows, embed[...], ((1,), (1,)))
        values = jnp.exp(spread * values * inv_rms(rows) * scale_row) * live
        values = values.astype(BF16)
        tiles[index] = values
        tiles_t[index] = values.astype(F32).T.astype(BF16)

    over(n // group, tile_chunk)

    def product(phase, u_turn):
        if u_turn is not None:
            for b in range(blocks):
                own_u = u_full[own_at(b, quarter), :]
                u_own_parts.append(own_u)
            own_us = u_own_parts[-blocks:]

            def send_u(d):
                s = peer(d)
                chosen = jnp.maximum(asked[s][0:1, :], 0.0)
                mixed = jnp.zeros((piece, comps), F32)
                for b in range(blocks):
                    mixed = mixed + jnp.where(chosen == float(b), 1.0, 0.0) * own_us[b].astype(F32)
                u_out[u_turn, s] = mixed.astype(BF16)
                to_rows(
                    u_out.at[u_turn, s], u_in.at[u_turn, me],
                    u_send.at[u_turn, s], u_recv.at[u_turn, me], s,
                ).start()

            over(n, send_u, 1)
            u_in[u_turn, me] = jnp.zeros((piece, comps), BF16)

        def reverse(index):
            result = dot(tiles[index], u_full[...], ((1,), (0,)))
            rev_out[phase, pl.ds(index * group, group)] = result.reshape(group, piece, comps)

        over(n // group, reverse)

        def send_rev(d):
            s = peer(d)
            to_rows(
                rev_out.at[phase, s], rev_in.at[phase, me],
                rev_send.at[phase, s], rev_recv.at[phase, me], s,
            ).start()

        over(n, send_rev, 1)
        if u_turn is None:
            u_mine = jnp.ones((own_rows, comps), BF16)
        else:
            u_mine = jnp.concatenate(own_us, axis=0)
        forward = dot(square[...], u_mine, ((1,), (0,)))
        if u_turn is not None:
            def u_got(d):
                s = peer(d)
                to_rows(
                    u_out.at[u_turn, s], u_in.at[u_turn, s],
                    u_send.at[u_turn, s], u_recv.at[u_turn, s], s,
                ).wait_recv()

            over(n, u_got, 1)

        def forward_chunk(index, sofar):
            if u_turn is None:
                fetched = jnp.ones((chunk, comps), BF16)
            else:
                fetched = u_in[u_turn, pl.ds(index * group, group)].reshape(chunk, comps)
            return sofar + dot(tiles_t[index], fetched, ((1,), (0,)))

        if n // group == 1:
            forward = forward_chunk(0, forward)
        else:
            forward = lax.fori_loop(0, n // group, forward_chunk, forward)
        for t in range(reps):
            for b in range(blocks):
                low = b * BLOCK + t * piece
                part_out[phase, t, b * piece:(b + 1) * piece] = forward[low:low + piece]
        for d in range(1, reps):
            t = rep_peer(d)
            to_rep(
                part_out.at[phase, t], part_in.at[phase, quarter],
                part_send.at[phase, t], part_recv.at[phase, quarter], t,
            ).start()
        placed[...] = part_out[phase, quarter]

        def place(d):
            s = peer(d)
            to_rows(
                rev_out.at[phase, s], rev_in.at[phase, s],
                rev_send.at[phase, s], rev_recv.at[phase, s], s,
            ).wait_recv()
            chosen = asked[s][0:1, :]
            value = rev_in[phase, s]
            for b in range(blocks):
                at = pl.ds(b * piece, piece)
                placed[at, :] = placed[at, :] + jnp.where(chosen == float(b), 1.0, 0.0) * value

        over(n, place, 1)
        result = placed[...]
        for d in range(1, reps):
            t = rep_peer(d)
            to_rep(
                part_out.at[phase, t], part_in.at[phase, t],
                part_send.at[phase, t], part_recv.at[phase, t], t,
            ).wait_recv()
            result = result + part_in[phase, t]
        return result

    def share(phase, values):
        y_own[phase] = values
        for d in range(1, reps):
            t = rep_peer(d)
            to_rep(
                y_own.at[phase], y_in.at[phase, quarter],
                y_send.at[phase, t], y_recv.at[phase, quarter], t,
            ).start()
        y_in[phase, quarter] = values

    def shared(phase):
        for d in range(1, reps):
            t = rep_peer(d)
            to_rep(
                y_own.at[phase], y_in.at[phase, t],
                y_send.at[phase, t], y_recv.at[phase, t], t,
            ).wait_recv()

    u_own_parts = []
    u_full[...] = jnp.ones((slab, comps), BF16)
    degree = product(0, None)
    share(0, degree)
    inv_own = lax.rsqrt(degree)
    shared(0)
    for t in range(reps):
        for b in range(blocks):
            low = b * BLOCK + t * piece
            inv[low:low + piece] = lax.rsqrt(y_in[0, t, b * piece:(b + 1) * piece])
    u_full[...] = (start[...].astype(F32) * inv[...]).astype(BF16)

    part = comps // reps
    sub_c = lax.broadcasted_iota(jnp.int32, (comps, comps), 0)
    lane_c = lax.broadcasted_iota(jnp.int32, (comps, comps), 1)
    sub_1 = lax.broadcasted_iota(jnp.int32, (comps, 1), 0)
    lane_1 = lax.broadcasted_iota(jnp.int32, (1, comps), 1)

    for turn in range(ITERS):
        phase = turn + 1
        y_mine = product(phase, turn) * inv_own
        partial = dot(y_mine.T, y_mine, ((1,), (0,)), HIGHEST)
        g_out[turn] = partial.reshape(reps, part, comps)
        for d in range(1, reps):
            t = rep_peer(d)
            to_rep(
                g_out.at[turn, t], g_in.at[turn, quarter],
                g_send.at[turn, t], g_recv.at[turn, quarter], t,
            ).start()
        share(phase, y_mine)
        slice_sum = g_out[turn, quarter]
        for d in range(1, reps):
            t = rep_peer(d)
            to_rep(
                g_out.at[turn, t], g_in.at[turn, t],
                g_send.at[turn, t], g_recv.at[turn, t], t,
            ).wait_recv()
            slice_sum = slice_sum + g_in[turn, t]
        slice_out[turn] = slice_sum
        slice_in[turn, me] = slice_sum

        def send_slice(d):
            s = peer(d)
            to_rows(
                slice_out.at[turn], slice_in.at[turn, me],
                slice_send.at[turn, s], slice_recv.at[turn, me], s,
            ).start()

        def slice_got(d):
            s = peer(d)
            to_rows(
                slice_out.at[turn], slice_in.at[turn, s],
                slice_send.at[turn, s], slice_recv.at[turn, s], s,
            ).wait_recv()

        over(n, send_slice, 1)
        over(n, slice_got, 1)
        slice_total = jnp.sum(slice_in[turn], axis=0)
        total_out[turn] = slice_total
        for d in range(1, reps):
            t = rep_peer(d)
            to_rep(
                total_out.at[turn], gram.at[turn, quarter],
                total_send.at[turn, t], total_recv.at[turn, quarter], t,
            ).start()
        gram[turn, quarter] = slice_total
        for d in range(1, reps):
            t = rep_peer(d)
            to_rep(
                total_out.at[turn], gram.at[turn, t],
                total_send.at[turn, t], total_recv.at[turn, t], t,
            ).wait_recv()

        elim[:, 0:comps] = gram[turn].reshape(comps, comps)
        elim[:, comps:2 * comps] = jnp.where(sub_c == lane_c, 1.0, 0.0)

        def eliminate(k, carry):
            row = elim[pl.ds(k, 1), :]
            left = elim[:, 0:comps]
            column = jnp.sum(jnp.where(lane_c == k, left, 0.0), axis=1, keepdims=True)
            pivot = jnp.sum(jnp.where(lane_1 == k, row[:, 0:comps], 0.0), axis=1, keepdims=True)
            factor = jnp.where(sub_1 > k, column / pivot, 0.0)
            elim[...] = elim[...] - factor * row
            return carry

        lax.fori_loop(0, comps, eliminate, 0)
        pivots = jnp.sum(
            jnp.where(sub_c == lane_c, elim[:, 0:comps], 0.0), axis=1, keepdims=True
        )
        lower_inv = elim[:, comps:2 * comps] * lax.rsqrt(pivots)
        shared(phase)
        last = turn == ITERS - 1
        for t in range(reps):
            fresh = dot(y_in[phase, t], lower_inv, ((1,), (1,)), HIGHEST)
            for b in range(blocks):
                low = b * BLOCK + t * piece
                rows = fresh[b * piece:(b + 1) * piece]
                if last:
                    out[low:low + piece] = rows * math.sqrt(slab * n)
                else:
                    u_full[low:low + piece] = (rows * inv[low:low + piece]).astype(BF16)

    def sent_rows(d):
        s = peer(d)
        link_copy(s).wait_send()
        to_rows(picks.at[s], pieces.at[me], embed_send.at[s], embed_recv.at[me], s).wait_send()
        for phase in range(ITERS + 1):
            to_rows(
                rev_out.at[phase, s], rev_in.at[phase, me],
                rev_send.at[phase, s], rev_recv.at[phase, me], s,
            ).wait_send()
        for turn in range(ITERS):
            to_rows(
                u_out.at[turn, s], u_in.at[turn, me],
                u_send.at[turn, s], u_recv.at[turn, me], s,
            ).wait_send()
            to_rows(
                slice_out.at[turn], slice_in.at[turn, me],
                slice_send.at[turn, s], slice_recv.at[turn, me], s,
            ).wait_send()

    over(n, sent_rows, 1)
    for d in range(1, reps):
        t = rep_peer(d)
        for phase in range(ITERS + 1):
            to_rep(
                part_out.at[phase, t], part_in.at[phase, quarter],
                part_send.at[phase, t], part_recv.at[phase, quarter], t,
            ).wait_send()
            to_rep(
                y_own.at[phase], y_in.at[phase, quarter],
                y_send.at[phase, t], y_recv.at[phase, quarter], t,
            ).wait_send()
        for turn in range(ITERS):
            to_rep(
                g_out.at[turn, t], g_in.at[turn, quarter],
                g_send.at[turn, t], g_recv.at[turn, quarter], t,
            ).wait_send()
            to_rep(
                total_out.at[turn], gram.at[turn, quarter],
                total_send.at[turn, t], total_recv.at[turn, quarter], t,
            ).wait_send()


def on_device(n, reps, embed, start, links):
    slab, features = embed.shape
    comps = start.shape[1]
    piece = BLOCK // reps
    own_rows = BLOCKS_DEV * piece
    part = comps // reps
    group = min(n, 8)
    phases = ITERS + 1
    wide = jnp.broadcast_to(
        jnp.pad(links, ((0, 0), (0, LANES - n)), constant_values=-1), (8, LANES)
    )
    vmem = pltpu.VMEM
    sem = pltpu.SemaphoreType.DMA
    scratch = [
        vmem((n, 8, LANES), jnp.int32),
        vmem((n, 8, LANES), F32),
        vmem((n, piece, LANES), F32),
        vmem((BLOCKS_DEV, piece, features), BF16),
        vmem((n, piece, features), BF16),
        vmem((n, piece, features), BF16),
        vmem((n // group, group * piece, slab), BF16),
        vmem((n // group, slab, group * piece), BF16),
        vmem((slab, own_rows), BF16),
        vmem((slab, comps), BF16),
        vmem((ITERS, n, piece, comps), BF16),
        vmem((ITERS, n, piece, comps), BF16),
        vmem((phases, n, piece, comps), F32),
        vmem((phases, n, piece, comps), F32),
        vmem((phases, reps, own_rows, comps), F32),
        vmem((phases, reps, own_rows, comps), F32),
        vmem((phases, own_rows, comps), F32),
        vmem((phases, reps, own_rows, comps), F32),
        vmem((slab, comps), F32),
        vmem((own_rows, comps), F32),
        vmem((ITERS, reps, part, comps), F32),
        vmem((ITERS, reps, part, comps), F32),
        vmem((ITERS, part, comps), F32),
        vmem((ITERS, n, part, comps), F32),
        vmem((ITERS, part, comps), F32),
        vmem((ITERS, reps, part, comps), F32),
        vmem((comps, 2 * comps), F32),
    ]
    sems = [
        (n,), (n,), (n,), (n,), (ITERS, n), (ITERS, n), (phases, n), (phases, n),
        (phases, reps), (phases, reps), (phases, reps), (phases, reps),
        (ITERS, reps), (ITERS, reps), (ITERS, n), (ITERS, n), (ITERS, reps), (ITERS, reps),
    ]
    return pl.pallas_call(
        functools.partial(kernel, n, reps),
        out_shape=jax.ShapeDtypeStruct((slab, comps), F32),
        in_specs=[pl.BlockSpec(memory_space=pltpu.VMEM)] * 3,
        out_specs=pl.BlockSpec(memory_space=pltpu.VMEM),
        scratch_shapes=scratch + [sem(shape) for shape in sems],
        compiler_params=pltpu.CompilerParams(
            collective_id=0, has_side_effects=True, vmem_limit_bytes=66 * 1000 * 1000
        ),
        name="spectral",
    )(embed, start, wide)


def solution(mesh):
    return jax.shard_map(
        functools.partial(on_device, mesh.shape["rows"], mesh.shape["rep"]),
        mesh=mesh,
        in_specs=(P("rows", None), P("rows", None), P("rows", None)),
        out_specs=P("rows", None),
        check_vma=False,
    )
```

```python
import functools
import math

import jax
import jax.numpy as jnp
from jax import lax
from jax.experimental import pallas as pl
from jax.experimental.pallas import tpu as pltpu
from jax.sharding import PartitionSpec as P

BLOCK = 128
BLOCKS_DEV = 4
ITERS = 2
LANES = 128
PANEL = 16
EPSILON = 1e-06
HIGHEST = lax.Precision.HIGHEST
F32 = jnp.float32
BF16 = jnp.bfloat16


def dot(a, b, dims, precision=None):
    return lax.dot_general(
        a, b, (dims, ((), ())), precision=precision, preferred_element_type=F32
    )


def inv_rms(rows):
    values = rows.astype(F32)
    return lax.rsqrt(jnp.mean(values * values, axis=1, keepdims=True) + EPSILON)


def as_row(column):
    return jnp.broadcast_to(column, (column.shape[0], LANES)).T[0:1, :]


def inverse_factor(matrix, inverse):
    size = matrix.shape[-1]
    count = size // PANEL
    per = matrix.shape[1] // PANEL
    sub = lax.broadcasted_iota(jnp.int32, (PANEL, size), 0)
    lane = lax.broadcasted_iota(jnp.int32, (PANEL, size), 1)
    left = [
        matrix[p // per, (p % per) * PANEL:(p % per + 1) * PANEL, :] for p in range(count)
    ]
    right = [jnp.where(lane == sub + p * PANEL, 1.0, 0.0) for p in range(count)]
    for p in range(count):
        low = p * PANEL
        columns = [
            jnp.broadcast_to(left[p][:, low + j:low + j + 1], (PANEL, size))
            for j in range(PANEL)
        ]
        rows, tracked = left[p], right[p]
        result = jnp.zeros((PANEL, size), F32)
        for k in range(PANEL):
            here = sub == k
            column = columns[k]
            pivot = jnp.broadcast_to(column[k:k + 1, :], (PANEL, size))
            result = jnp.where(here, tracked * lax.rsqrt(pivot), result)
            scale = 1.0 / pivot

            def cleared(values):
                row = values[k:k + 1, :] * scale
                return jnp.where(here, row, values - column * row)

            rows, tracked = cleared(rows), cleared(tracked)
            for j in range(k + 1, PANEL):
                columns[j] = cleared(columns[j])
        for below in range(p + 1, count):
            base = left[below]
            for j in range(PANEL):
                column = base[:, low + j:low + j + 1]
                right[below] = right[below] - column * tracked[j:j + 1, :]
                left[below] = left[below] - column * rows[j:j + 1, :]
        inverse[low:low + PANEL, :] = result


def kernel(
    n, reps,
    embed_hbm, start_hbm, links, out,
    embed, start, link_out, link_in, asked, alive, own, picks, pieces, tiles, tiles_t, square,
    u_full, u_out, u_in, rev_out, rev_in, part_out, part_in, y_own, y_in, inv, placed,
    g_out, g_in, slice_out, slice_in, total_out, gram, elim,
    back_out, back_in, back_sum, degree_out, degree_in,
    link_send, link_recv, embed_send, embed_recv, u_send, u_recv, rev_send, rev_recv,
    part_send, part_recv, y_send, y_recv, g_send, g_recv, slice_send, slice_recv,
    total_send, total_recv, load_sem, degree_send, degree_recv,
):
    me = lax.axis_index("rows")
    quarter = lax.axis_index("rep")
    slab, features = embed.shape
    comps = start.shape[1]
    blocks = BLOCKS_DEV
    piece = BLOCK // reps
    own_rows = blocks * piece
    spread = 2.0 / math.sqrt(features)
    group = min(n, 8)
    chunk = group * piece
    unroll = n <= 8

    def over(count, body, low=0):
        if unroll:
            for index in range(low, count):
                body(index)
        else:
            def step(index, carry):
                body(index)
                return carry
            lax.fori_loop(low, count, step, 0)

    def peer(distance):
        return lax.rem(me + distance, n)

    def rep_peer(distance):
        return lax.rem(quarter + distance, reps)

    def to_rows(src, dst, send, recv, target):
        return pltpu.make_async_remote_copy(
            src_ref=src, dst_ref=dst, send_sem=send, recv_sem=recv,
            device_id={"rows": target}, device_id_type=pl.DeviceIdType.MESH,
        )

    def to_rep(src, dst, send, recv, target):
        return pltpu.make_async_remote_copy(
            src_ref=src, dst_ref=dst, send_sem=send, recv_sem=recv,
            device_id={"rep": target}, device_id_type=pl.DeviceIdType.MESH,
        )

    def own_at(block, which):
        return pl.ds(pl.multiple_of(block * BLOCK + which * piece, piece), piece)

    load_embed = pltpu.make_async_copy(embed_hbm, embed, load_sem.at[0])
    load_start = pltpu.make_async_copy(start_hbm, start, load_sem.at[1])
    load_embed.start()
    load_start.start()
    link_out[...] = jnp.full((8, LANES), -1, jnp.int32)
    link_out[0:1, 0:n] = links[...]
    barrier = pltpu.get_barrier_semaphore()

    def greet(distance):
        pl.semaphore_signal(
            barrier, inc=1, device_id={"rows": peer(distance)},
            device_id_type=pl.DeviceIdType.MESH,
        )

    over(n, greet, 1)
    for distance in range(1, reps):
        pl.semaphore_signal(
            barrier, inc=1, device_id={"rep": rep_peer(distance)},
            device_id_type=pl.DeviceIdType.MESH,
        )
    pl.semaphore_wait(barrier, n + reps - 2)

    def link_copy(s):
        return to_rows(link_out, link_in.at[me], link_send.at[s], link_recv.at[me], s)

    def link_got(s):
        return to_rows(link_out, link_in.at[s], link_send.at[s], link_recv.at[s], s)

    over(n, lambda d: link_copy(peer(d)).start(), 1)
    lane = lax.broadcasted_iota(jnp.int32, (8, LANES), 1)
    pieces[me] = jnp.zeros((piece, features), BF16)

    load_embed.wait()
    load_start.wait()
    for b in range(blocks):
        own[b] = embed[own_at(b, quarter), :]
    own_flat = own[...].reshape(own_rows, features)
    own_scale = inv_rms(own_flat)
    slab_scale = jnp.concatenate(
        [inv_rms(embed[b * BLOCK:(b + 1) * BLOCK, :]) for b in range(blocks)], axis=0
    )
    scale_row = as_row(slab_scale)

    def alive_of(s):
        entry = jnp.sum(jnp.where(lane == s, link_out[...], 0).astype(F32), axis=1, keepdims=True)
        alive[s] = jnp.broadcast_to(
            jnp.where(entry[0:1] >= 0.0, 1.0, 0.0), (piece, LANES)
        )

    over(n, alive_of)

    def pick(d):
        s = peer(d)
        link_got(s).wait_recv()
        entry = jnp.sum(
            jnp.where(lane == me, link_in[s], 0).astype(F32), axis=1, keepdims=True
        )
        asked[s] = jnp.broadcast_to(entry, (8, LANES))
        chosen = jnp.maximum(entry[0:1], 0.0)
        mixed = jnp.zeros((piece, features), F32)
        for b in range(blocks):
            mixed = mixed + jnp.where(chosen == float(b), 1.0, 0.0) * own[b].astype(F32)
        picks[s] = mixed.astype(BF16)
        to_rows(picks.at[s], pieces.at[me], embed_send.at[s], embed_recv.at[me], s).start()

    over(n, pick, 1)

    products = dot(embed[...], own_flat, ((1,), (1,)))
    affinity = jnp.exp(spread * products * slab_scale * as_row(own_scale))
    row_id = lax.broadcasted_iota(jnp.int32, (slab, own_rows), 0)
    col_id = lax.broadcasted_iota(jnp.int32, (slab, own_rows), 1)
    col_row = (col_id // piece) * BLOCK + quarter * piece + col_id % piece
    square[...] = jnp.where(row_id == col_row, 0.0, affinity).astype(BF16)

    def embed_got(d):
        s = peer(d)
        to_rows(picks.at[s], pieces.at[s], embed_send.at[s], embed_recv.at[s], s).wait_recv()

    over(n, embed_got, 1)

    def tile_chunk(index):
        first = index * group
        rows = pieces[pl.ds(first, group)].reshape(chunk, features)
        live = alive[pl.ds(first, group)].reshape(chunk, LANES)[:, 0:1]
        values = dot(rows, embed[...], ((1,), (1,)))
        values = jnp.exp(spread * values * inv_rms(rows) * scale_row) * live
        values = values.astype(BF16)
        tiles[index] = values
        tiles_t[index] = values.astype(F32).T.astype(BF16)

    over(n // group, tile_chunk)

    def product(phase, u_turn):
        own_us = [u_full[own_at(b, quarter), :] for b in range(blocks)]

        def send_u(d):
            s = peer(d)
            chosen = jnp.maximum(asked[s][0:1, :], 0.0)
            mixed = jnp.zeros((piece, comps), F32)
            for b in range(blocks):
                mixed = mixed + jnp.where(chosen == float(b), 1.0, 0.0) * own_us[b].astype(F32)
            u_out[u_turn, s] = mixed.astype(BF16)
            to_rows(
                u_out.at[u_turn, s], u_in.at[u_turn, me],
                u_send.at[u_turn, s], u_recv.at[u_turn, me], s,
            ).start()

        over(n, send_u, 1)
        u_in[u_turn, me] = jnp.zeros((piece, comps), BF16)

        def reverse(index):
            result = dot(tiles[index], u_full[...], ((1,), (0,)))
            rev_out[phase, pl.ds(index * group, group)] = result.reshape(group, piece, comps)

        over(n // group, reverse)

        def send_rev(d):
            s = peer(d)
            to_rows(
                rev_out.at[phase, s], rev_in.at[phase, me],
                rev_send.at[phase, s], rev_recv.at[phase, me], s,
            ).start()

        over(n, send_rev, 1)
        u_mine = jnp.concatenate(own_us, axis=0)
        forward = dot(square[...], u_mine, ((1,), (0,)))

        def u_got(d):
            s = peer(d)
            to_rows(
                u_out.at[u_turn, s], u_in.at[u_turn, s],
                u_send.at[u_turn, s], u_recv.at[u_turn, s], s,
            ).wait_recv()

        over(n, u_got, 1)

        def forward_chunk(index, sofar):
            fetched = u_in[u_turn, pl.ds(index * group, group)].reshape(chunk, comps)
            return sofar + dot(tiles_t[index], fetched, ((1,), (0,)))

        if n // group == 1:
            forward = forward_chunk(0, forward)
        else:
            forward = lax.fori_loop(0, n // group, forward_chunk, forward)
        for t in range(reps):
            for b in range(blocks):
                low = b * BLOCK + t * piece
                part_out[phase, t, b * piece:(b + 1) * piece] = forward[low:low + piece]
        for d in range(1, reps):
            t = rep_peer(d)
            to_rep(
                part_out.at[phase, t], part_in.at[phase, quarter],
                part_send.at[phase, t], part_recv.at[phase, quarter], t,
            ).start()
        placed[...] = part_out[phase, quarter]

        def place(d):
            s = peer(d)
            to_rows(
                rev_out.at[phase, s], rev_in.at[phase, s],
                rev_send.at[phase, s], rev_recv.at[phase, s], s,
            ).wait_recv()
            chosen = asked[s][0:1, :]
            value = rev_in[phase, s]
            for b in range(blocks):
                at = pl.ds(b * piece, piece)
                placed[at, :] = placed[at, :] + jnp.where(chosen == float(b), 1.0, 0.0) * value

        over(n, place, 1)
        result = placed[...]
        for d in range(1, reps):
            t = rep_peer(d)
            to_rep(
                part_out.at[phase, t], part_in.at[phase, t],
                part_send.at[phase, t], part_recv.at[phase, t], t,
            ).wait_recv()
            result = result + part_in[phase, t]
        return result

    def share(phase, values):
        y_own[phase] = values
        for d in range(1, reps):
            t = rep_peer(d)
            to_rep(
                y_own.at[phase], y_in.at[phase, quarter],
                y_send.at[phase, t], y_recv.at[phase, quarter], t,
            ).start()
        y_in[phase, quarter] = values

    def shared(phase):
        for d in range(1, reps):
            t = rep_peer(d)
            to_rep(
                y_own.at[phase], y_in.at[phase, t],
                y_send.at[phase, t], y_recv.at[phase, t], t,
            ).wait_recv()

    def back_chunk(index):
        sums = dot(jnp.ones((8, slab), BF16), tiles_t[index], ((1,), (0,)))
        for g in range(group):
            back_out[index * group + g, :, 0:piece] = sums[:, g * piece:(g + 1) * piece]

    def send_back(d):
        s = peer(d)
        to_rows(back_out.at[s], back_in.at[me], rev_send.at[0, s], rev_recv.at[0, me], s).start()

    def back_got(d):
        s = peer(d)
        to_rows(
            back_out.at[s], back_in.at[s], rev_send.at[0, s], rev_recv.at[0, s], s
        ).wait_recv()
        value = back_in[s]
        for b in range(blocks):
            back_sum[b] = back_sum[b] + jnp.where(asked[s] == float(b), 1.0, 0.0) * value

    back_out[...] = jnp.zeros_like(back_out)
    over(n // group, back_chunk)
    over(n, send_back, 1)
    back_sum[...] = jnp.zeros_like(back_sum)
    degree_out[...] = dot(jnp.ones((8, own_rows), BF16), square[...], ((1,), (1,)))

    def own_chunk(index):
        degree_out[...] = degree_out[...] + dot(
            jnp.ones((8, chunk), BF16), tiles[index], ((1,), (0,))
        )

    over(n // group, own_chunk)
    over(n, back_got, 1)
    for b in range(blocks):
        at = pl.ds(b * BLOCK, BLOCK)
        degree_out[:, at] = degree_out[:, at] + pltpu.roll(back_sum[b], quarter * piece, 1)

    def degree_copy(t):
        return to_rep(
            degree_out, degree_in.at[quarter], degree_send.at[t], degree_recv.at[quarter], t
        )

    for d in range(1, reps):
        degree_copy(rep_peer(d)).start()
    degree_in[quarter] = degree_out[...]
    for d in range(1, reps):
        t = rep_peer(d)
        to_rep(
            degree_out, degree_in.at[t], degree_send.at[t], degree_recv.at[t], t
        ).wait_recv()
    inv_row = lax.rsqrt(jnp.sum(degree_in[...], axis=0))[0:1]
    for b in range(blocks):
        inv[b * BLOCK:(b + 1) * BLOCK] = jnp.broadcast_to(
            inv_row[:, b * BLOCK:(b + 1) * BLOCK], (LANES, BLOCK)
        ).T
    inv_own = jnp.concatenate([inv[own_at(b, quarter), 0:comps] for b in range(blocks)], axis=0)
    u_full[...] = (start[...].astype(F32) * inv[...]).astype(BF16)

    part = comps // reps
    for turn in range(ITERS):
        phase = turn + 1
        y_mine = product(phase, turn) * inv_own
        partial = dot(y_mine.T, y_mine, ((1,), (0,)), HIGHEST)
        g_out[turn] = partial.reshape(reps, part, comps)
        for d in range(1, reps):
            t = rep_peer(d)
            to_rep(
                g_out.at[turn, t], g_in.at[turn, quarter],
                g_send.at[turn, t], g_recv.at[turn, quarter], t,
            ).start()
        share(phase, y_mine)
        slice_sum = g_out[turn, quarter]
        for d in range(1, reps):
            t = rep_peer(d)
            to_rep(
                g_out.at[turn, t], g_in.at[turn, t],
                g_send.at[turn, t], g_recv.at[turn, t], t,
            ).wait_recv()
            slice_sum = slice_sum + g_in[turn, t]
        slice_out[turn] = slice_sum
        slice_in[turn, me] = slice_sum

        def send_slice(d):
            s = peer(d)
            to_rows(
                slice_out.at[turn], slice_in.at[turn, me],
                slice_send.at[turn, s], slice_recv.at[turn, me], s,
            ).start()

        def slice_got(d):
            s = peer(d)
            to_rows(
                slice_out.at[turn], slice_in.at[turn, s],
                slice_send.at[turn, s], slice_recv.at[turn, s], s,
            ).wait_recv()

        over(n, send_slice, 1)
        over(n, slice_got, 1)
        slice_total = jnp.sum(slice_in[turn], axis=0)
        total_out[turn] = slice_total
        for d in range(1, reps):
            t = rep_peer(d)
            to_rep(
                total_out.at[turn], gram.at[turn, quarter],
                total_send.at[turn, t], total_recv.at[turn, quarter], t,
            ).start()
        gram[turn, quarter] = slice_total
        for d in range(1, reps):
            t = rep_peer(d)
            to_rep(
                total_out.at[turn], gram.at[turn, t],
                total_send.at[turn, t], total_recv.at[turn, t], t,
            ).wait_recv()

        inverse_factor(gram.at[turn], elim)
        lower_inv = elim[...]
        shared(phase)
        last = turn == ITERS - 1
        for t in range(reps):
            fresh = dot(y_in[phase, t], lower_inv, ((1,), (1,)), HIGHEST)
            for b in range(blocks):
                low = b * BLOCK + t * piece
                rows = fresh[b * piece:(b + 1) * piece]
                if last:
                    out[low:low + piece] = rows * math.sqrt(slab * n)
                else:
                    u_full[low:low + piece] = (rows * inv[low:low + piece]).astype(BF16)

    def sent_rows(d):
        s = peer(d)
        link_copy(s).wait_send()
        to_rows(picks.at[s], pieces.at[me], embed_send.at[s], embed_recv.at[me], s).wait_send()
        to_rows(back_out.at[s], back_in.at[me], rev_send.at[0, s], rev_recv.at[0, me], s).wait_send()
        for phase in range(1, ITERS + 1):
            to_rows(
                rev_out.at[phase, s], rev_in.at[phase, me],
                rev_send.at[phase, s], rev_recv.at[phase, me], s,
            ).wait_send()
        for turn in range(ITERS):
            to_rows(
                u_out.at[turn, s], u_in.at[turn, me],
                u_send.at[turn, s], u_recv.at[turn, me], s,
            ).wait_send()
            to_rows(
                slice_out.at[turn], slice_in.at[turn, me],
                slice_send.at[turn, s], slice_recv.at[turn, me], s,
            ).wait_send()

    over(n, sent_rows, 1)
    for d in range(1, reps):
        t = rep_peer(d)
        degree_copy(t).wait_send()
        for phase in range(1, ITERS + 1):
            to_rep(
                part_out.at[phase, t], part_in.at[phase, quarter],
                part_send.at[phase, t], part_recv.at[phase, quarter], t,
            ).wait_send()
            to_rep(
                y_own.at[phase], y_in.at[phase, quarter],
                y_send.at[phase, t], y_recv.at[phase, quarter], t,
            ).wait_send()
        for turn in range(ITERS):
            to_rep(
                g_out.at[turn, t], g_in.at[turn, quarter],
                g_send.at[turn, t], g_recv.at[turn, quarter], t,
            ).wait_send()
            to_rep(
                total_out.at[turn], gram.at[turn, quarter],
                total_send.at[turn, t], total_recv.at[turn, quarter], t,
            ).wait_send()


def on_device(n, reps, embed, start, links):
    slab, features = embed.shape
    comps = start.shape[1]
    piece = BLOCK // reps
    own_rows = BLOCKS_DEV * piece
    part = comps // reps
    group = min(n, 8)
    phases = ITERS + 1
    vmem = pltpu.VMEM
    sem = pltpu.SemaphoreType.DMA
    scratch = [
        vmem((slab, features), BF16),
        vmem((slab, comps), BF16),
        vmem((8, LANES), jnp.int32),
        vmem((n, 8, LANES), jnp.int32),
        vmem((n, 8, LANES), F32),
        vmem((n, piece, LANES), F32),
        vmem((BLOCKS_DEV, piece, features), BF16),
        vmem((n, piece, features), BF16),
        vmem((n, piece, features), BF16),
        vmem((n // group, group * piece, slab), BF16),
        vmem((n // group, slab, group * piece), BF16),
        vmem((slab, own_rows), BF16),
        vmem((slab, comps), BF16),
        vmem((ITERS, n, piece, comps), BF16),
        vmem((ITERS, n, piece, comps), BF16),
        vmem((phases, n, piece, comps), F32),
        vmem((phases, n, piece, comps), F32),
        vmem((phases, reps, own_rows, comps), F32),
        vmem((phases, reps, own_rows, comps), F32),
        vmem((phases, own_rows, comps), F32),
        vmem((phases, reps, own_rows, comps), F32),
        vmem((slab, comps), F32),
        vmem((own_rows, comps), F32),
        vmem((ITERS, reps, part, comps), F32),
        vmem((ITERS, reps, part, comps), F32),
        vmem((ITERS, part, comps), F32),
        vmem((ITERS, n, part, comps), F32),
        vmem((ITERS, part, comps), F32),
        vmem((ITERS, reps, part, comps), F32),
        vmem((comps, comps), F32),
        vmem((n, 8, LANES), F32),
        vmem((n, 8, LANES), F32),
        vmem((BLOCKS_DEV, 8, LANES), F32),
        vmem((8, slab), F32),
        vmem((reps, 8, slab), F32),
    ]
    sems = [
        (n,), (n,), (n,), (n,), (ITERS, n), (ITERS, n), (phases, n), (phases, n),
        (phases, reps), (phases, reps), (phases, reps), (phases, reps),
        (ITERS, reps), (ITERS, reps), (ITERS, n), (ITERS, n), (ITERS, reps), (ITERS, reps),
        (2,), (reps,), (reps,),
    ]
    return pl.pallas_call(
        functools.partial(kernel, n, reps),
        out_shape=jax.ShapeDtypeStruct((slab, comps), F32),
        in_specs=[pl.BlockSpec(memory_space=pl.ANY)] * 2 + [pl.BlockSpec(memory_space=pltpu.VMEM)],
        out_specs=pl.BlockSpec(memory_space=pltpu.VMEM),
        scratch_shapes=scratch + [sem(shape) for shape in sems],
        compiler_params=pltpu.CompilerParams(
            collective_id=0, has_side_effects=True, vmem_limit_bytes=66 * 1000 * 1000
        ),
        name="spectral",
    )(embed, start, links)


def solution(mesh):
    return jax.shard_map(
        functools.partial(on_device, mesh.shape["rows"], mesh.shape["rep"]),
        mesh=mesh,
        in_specs=(P("rows", None), P("rows", None), P("rows", None)),
        out_specs=P("rows", None),
        check_vma=False,
    )
```

```python
import functools
import math

import jax
import jax.numpy as jnp
from jax import lax
from jax.experimental import pallas as pl
from jax.experimental.pallas import tpu as pltpu
from jax.sharding import PartitionSpec as P

BLOCK = 128
BLOCKS_DEV = 4
ITERS = 2
LANES = 128
PANEL = 16
EPSILON = 1e-06
HIGHEST = lax.Precision.HIGHEST
F32 = jnp.float32
BF16 = jnp.bfloat16


def dot(a, b, dims, precision=None):
    return lax.dot_general(
        a, b, (dims, ((), ())), precision=precision, preferred_element_type=F32
    )


def inv_rms(rows):
    values = rows.astype(F32)
    return lax.rsqrt(jnp.mean(values * values, axis=1, keepdims=True) + EPSILON)


def as_row(column):
    return jnp.broadcast_to(column, (column.shape[0], LANES)).T[0:1, :]


def inverse_factor(matrix, inverse):
    size = matrix.shape[-1]
    count = size // PANEL
    per = matrix.shape[1] // PANEL
    sub = lax.broadcasted_iota(jnp.int32, (PANEL, size), 0)
    lane = lax.broadcasted_iota(jnp.int32, (PANEL, size), 1)
    left = [
        matrix[p // per, (p % per) * PANEL:(p % per + 1) * PANEL, :] for p in range(count)
    ]
    right = [jnp.where(lane == sub + p * PANEL, 1.0, 0.0) for p in range(count)]
    for p in range(count):
        low = p * PANEL
        columns = [
            jnp.broadcast_to(left[p][:, low + j:low + j + 1], (PANEL, size))
            for j in range(PANEL)
        ]
        rows, tracked = left[p], right[p]
        result = jnp.zeros((PANEL, size), F32)
        for k in range(PANEL):
            here = sub == k
            column = columns[k]
            pivot = jnp.broadcast_to(column[k:k + 1, :], (PANEL, size))
            result = jnp.where(here, tracked * lax.rsqrt(pivot), result)
            scale = 1.0 / pivot

            def cleared(values):
                row = values[k:k + 1, :] * scale
                return jnp.where(here, row, values - column * row)

            rows, tracked = cleared(rows), cleared(tracked)
            for j in range(k + 1, PANEL):
                columns[j] = cleared(columns[j])
        for below in range(p + 1, count):
            base = left[below]
            for j in range(PANEL):
                column = base[:, low + j:low + j + 1]
                right[below] = right[below] - column * tracked[j:j + 1, :]
                left[below] = left[below] - column * rows[j:j + 1, :]
        inverse[low:low + PANEL, :] = result


def kernel(
    n, reps,
    embed_hbm, start_hbm, links, out,
    embed, start, link_out, link_in, asked, alive, own, picks, pieces, tiles, tiles_t, square,
    u_full, u_out, u_in, rev_out, rev_in, part_out, part_in, y_own, y_in, inv, placed,
    g_out, g_in, slice_out, slice_in, total_out, gram, elim,
    back_out, back_in, back_sum, degree_out, degree_in,
    link_send, link_recv, embed_send, embed_recv, u_send, u_recv, rev_send, rev_recv,
    part_send, part_recv, y_send, y_recv, g_send, g_recv, slice_send, slice_recv,
    total_send, total_recv, load_sem, degree_send, degree_recv,
):
    me = lax.axis_index("rows")
    quarter = lax.axis_index("rep")
    slab, features = embed.shape
    comps = start.shape[1]
    blocks = BLOCKS_DEV
    piece = BLOCK // reps
    own_rows = blocks * piece
    spread = 2.0 / math.sqrt(features)
    group = max(1, min(n, LANES // piece))
    chunk = group * piece
    unroll = n <= 8

    def over(count, body, low=0):
        if unroll:
            for index in range(low, count):
                body(index)
        else:
            def step(index, carry):
                body(index)
                return carry
            lax.fori_loop(low, count, step, 0)

    def peer(distance):
        return lax.rem(me + distance, n)

    def rep_peer(distance):
        return lax.rem(quarter + distance, reps)

    def to_rows(src, dst, send, recv, target):
        return pltpu.make_async_remote_copy(
            src_ref=src, dst_ref=dst, send_sem=send, recv_sem=recv,
            device_id={"rows": target}, device_id_type=pl.DeviceIdType.MESH,
        )

    def to_rep(src, dst, send, recv, target):
        return pltpu.make_async_remote_copy(
            src_ref=src, dst_ref=dst, send_sem=send, recv_sem=recv,
            device_id={"rep": target}, device_id_type=pl.DeviceIdType.MESH,
        )

    def own_at(block, which):
        return pl.ds(pl.multiple_of(block * BLOCK + which * piece, piece), piece)

    load_embed = pltpu.make_async_copy(embed_hbm, embed, load_sem.at[0])
    load_start = pltpu.make_async_copy(start_hbm, start, load_sem.at[1])
    load_embed.start()
    load_start.start()
    link_out[...] = jnp.full((8, LANES), -1, jnp.int32)
    link_out[0:1, 0:n] = links[...]
    barrier = pltpu.get_barrier_semaphore()

    def greet(distance):
        pl.semaphore_signal(
            barrier, inc=1, device_id={"rows": peer(distance)},
            device_id_type=pl.DeviceIdType.MESH,
        )

    over(n, greet, 1)
    for distance in range(1, reps):
        pl.semaphore_signal(
            barrier, inc=1, device_id={"rep": rep_peer(distance)},
            device_id_type=pl.DeviceIdType.MESH,
        )
    pl.semaphore_wait(barrier, n + reps - 2)

    def link_copy(d):
        return to_rows(link_out, link_in.at[n - d], link_send.at[d], link_recv.at[n - d], peer(d))

    def link_got(d):
        return to_rows(link_out, link_in.at[d], link_send.at[d], link_recv.at[d], peer(d))

    over(n, lambda d: link_copy(d).start(), 1)
    lane = lax.broadcasted_iota(jnp.int32, (8, LANES), 1)
    pieces[0] = jnp.zeros((piece, features), BF16)

    load_embed.wait()
    load_start.wait()
    for b in range(blocks):
        own[b] = embed[own_at(b, quarter), :]
    own_flat = own[...].reshape(own_rows, features)
    own_scale = inv_rms(own_flat)
    slab_scale = jnp.concatenate(
        [inv_rms(embed[b * BLOCK:(b + 1) * BLOCK, :]) for b in range(blocks)], axis=0
    )
    scale_row = as_row(slab_scale)

    def alive_of(d):
        entry = jnp.sum(jnp.where(lane == peer(d), link_out[...], 0).astype(F32), axis=1, keepdims=True)
        alive[d] = jnp.broadcast_to(
            jnp.where(entry[0:1] >= 0.0, 1.0, 0.0), (piece, LANES)
        )

    over(n, alive_of)

    def pick(d):
        s = peer(d)
        link_got(d).wait_recv()
        entry = jnp.sum(
            jnp.where(lane == me, link_in[d], 0).astype(F32), axis=1, keepdims=True
        )
        asked[d] = jnp.broadcast_to(entry, (8, LANES))
        chosen = jnp.maximum(entry[0:1], 0.0)
        mixed = jnp.zeros((piece, features), F32)
        for b in range(blocks):
            mixed = mixed + jnp.where(chosen == float(b), 1.0, 0.0) * own[b].astype(F32)
        picks[d] = mixed.astype(BF16)
        to_rows(picks.at[d], pieces.at[n - d], embed_send.at[d], embed_recv.at[n - d], s).start()

    over(n, pick, 1)

    products = dot(embed[...], own_flat, ((1,), (1,)))
    affinity = jnp.exp(spread * products * slab_scale * as_row(own_scale))
    row_id = lax.broadcasted_iota(jnp.int32, (slab, own_rows), 0)
    col_id = lax.broadcasted_iota(jnp.int32, (slab, own_rows), 1)
    col_row = (col_id // piece) * BLOCK + quarter * piece + col_id % piece
    square[...] = jnp.where(row_id == col_row, 0.0, affinity).astype(BF16)

    def embed_got(d):
        s = peer(d)
        to_rows(picks.at[d], pieces.at[d], embed_send.at[d], embed_recv.at[d], s).wait_recv()


    def tile_chunk(turned):
        index = n // group - 1 - turned
        first = index * group
        if unroll:
            for g in range(group - 1, -1, -1):
                if first + g:
                    embed_got(first + g)
        rows = pieces[pl.ds(first, group)].reshape(chunk, features)
        live = alive[pl.ds(first, group)].reshape(chunk, LANES)[:, 0:1]
        values = dot(rows, embed[...], ((1,), (1,)))
        values = jnp.exp(spread * values * inv_rms(rows) * scale_row) * live
        values = values.astype(BF16)
        tiles[index] = values
        tiles_t[index] = values.astype(F32).T.astype(BF16)

    if not unroll:
        over(n, embed_got, 1)
    over(n // group, tile_chunk)

    def product(phase, u_turn):
        own_us = [u_full[own_at(b, quarter), :] for b in range(blocks)]

        def send_u(d):
            s = peer(d)
            chosen = jnp.maximum(asked[d][0:1, :], 0.0)
            mixed = jnp.zeros((piece, comps), F32)
            for b in range(blocks):
                mixed = mixed + jnp.where(chosen == float(b), 1.0, 0.0) * own_us[b].astype(F32)
            u_out[u_turn, d] = mixed.astype(BF16)
            to_rows(
                u_out.at[u_turn, d], u_in.at[u_turn, n - d],
                u_send.at[u_turn, d], u_recv.at[u_turn, n - d], s,
            ).start()

        over(n, send_u, 1)
        u_in[u_turn, 0] = jnp.zeros((piece, comps), BF16)

        def reverse(index):
            result = dot(tiles[index], u_full[...], ((1,), (0,)))
            rev_out[phase, pl.ds(index * group, group)] = result.reshape(group, piece, comps)

        over(n // group, reverse)

        def send_rev(d):
            s = peer(d)
            to_rows(
                rev_out.at[phase, d], rev_in.at[phase, n - d],
                rev_send.at[phase, d], rev_recv.at[phase, n - d], s,
            ).start()

        over(n, send_rev, 1)
        u_mine = jnp.concatenate(own_us, axis=0)
        forward = dot(square[...], u_mine, ((1,), (0,)))

        def u_got(d):
            s = peer(d)
            to_rows(
                u_out.at[u_turn, d], u_in.at[u_turn, d],
                u_send.at[u_turn, d], u_recv.at[u_turn, d], s,
            ).wait_recv()

        over(n, u_got, 1)

        def forward_chunk(index, sofar):
            fetched = u_in[u_turn, pl.ds(index * group, group)].reshape(chunk, comps)
            return sofar + dot(tiles_t[index], fetched, ((1,), (0,)))

        if unroll:
            for index in range(n // group):
                forward = forward_chunk(index, forward)
        else:
            forward = lax.fori_loop(0, n // group, forward_chunk, forward)
        for t in range(reps):
            for b in range(blocks):
                low = b * BLOCK + t * piece
                part_out[phase, t, b * piece:(b + 1) * piece] = forward[low:low + piece]
        for d in range(1, reps):
            t = rep_peer(d)
            to_rep(
                part_out.at[phase, t], part_in.at[phase, quarter],
                part_send.at[phase, t], part_recv.at[phase, quarter], t,
            ).start()
        placed[...] = part_out[phase, quarter]

        def place(d):
            s = peer(d)
            to_rows(
                rev_out.at[phase, d], rev_in.at[phase, d],
                rev_send.at[phase, d], rev_recv.at[phase, d], s,
            ).wait_recv()
            chosen = asked[d][0:1, :]
            value = rev_in[phase, d]
            for b in range(blocks):
                at = pl.ds(b * piece, piece)
                placed[at, :] = placed[at, :] + jnp.where(chosen == float(b), 1.0, 0.0) * value

        over(n, place, 1)
        result = placed[...]
        for d in range(1, reps):
            t = rep_peer(d)
            to_rep(
                part_out.at[phase, t], part_in.at[phase, t],
                part_send.at[phase, t], part_recv.at[phase, t], t,
            ).wait_recv()
            result = result + part_in[phase, t]
        return result

    def share(phase, values):
        y_own[phase] = values
        for d in range(1, reps):
            t = rep_peer(d)
            to_rep(
                y_own.at[phase], y_in.at[phase, quarter],
                y_send.at[phase, t], y_recv.at[phase, quarter], t,
            ).start()
        y_in[phase, quarter] = values

    def shared(phase):
        for d in range(1, reps):
            t = rep_peer(d)
            to_rep(
                y_own.at[phase], y_in.at[phase, t],
                y_send.at[phase, t], y_recv.at[phase, t], t,
            ).wait_recv()

    def back_chunk(index):
        sums = dot(jnp.ones((8, slab), BF16), tiles_t[index], ((1,), (0,)))
        for g in range(group):
            back_out[index * group + g, :, 0:piece] = sums[:, g * piece:(g + 1) * piece]

    def send_back(d):
        s = peer(d)
        to_rows(back_out.at[d], back_in.at[n - d], rev_send.at[0, d], rev_recv.at[0, n - d], s).start()

    def back_got(d):
        s = peer(d)
        to_rows(
            back_out.at[d], back_in.at[d], rev_send.at[0, d], rev_recv.at[0, d], s
        ).wait_recv()
        value = back_in[d]
        for b in range(blocks):
            back_sum[b] = back_sum[b] + jnp.where(asked[d] == float(b), 1.0, 0.0) * value

    back_out[...] = jnp.zeros_like(back_out)
    over(n // group, back_chunk)
    over(n, send_back, 1)
    back_sum[...] = jnp.zeros_like(back_sum)
    degree_out[...] = dot(jnp.ones((8, own_rows), BF16), square[...], ((1,), (1,)))

    def own_chunk(index):
        degree_out[...] = degree_out[...] + dot(
            jnp.ones((8, chunk), BF16), tiles[index], ((1,), (0,))
        )

    over(n // group, own_chunk)
    over(n, back_got, 1)
    for b in range(blocks):
        at = pl.ds(b * BLOCK, BLOCK)
        degree_out[:, at] = degree_out[:, at] + pltpu.roll(back_sum[b], quarter * piece, 1)

    def degree_copy(t):
        return to_rep(
            degree_out, degree_in.at[quarter], degree_send.at[t], degree_recv.at[quarter], t
        )

    for d in range(1, reps):
        degree_copy(rep_peer(d)).start()
    degree_in[quarter] = degree_out[...]
    for d in range(1, reps):
        t = rep_peer(d)
        to_rep(
            degree_out, degree_in.at[t], degree_send.at[t], degree_recv.at[t], t
        ).wait_recv()
    inv_row = lax.rsqrt(jnp.sum(degree_in[...], axis=0))[0:1]
    for b in range(blocks):
        inv[b * BLOCK:(b + 1) * BLOCK] = jnp.broadcast_to(
            inv_row[:, b * BLOCK:(b + 1) * BLOCK], (LANES, BLOCK)
        ).T
    inv_own = jnp.concatenate([inv[own_at(b, quarter), 0:comps] for b in range(blocks)], axis=0)
    u_full[...] = (start[...].astype(F32) * inv[...]).astype(BF16)

    part = comps // reps
    for turn in range(ITERS):
        phase = turn + 1
        y_mine = product(phase, turn) * inv_own
        partial = dot(y_mine.T, y_mine, ((1,), (0,)), HIGHEST)
        g_out[turn] = partial.reshape(reps, part, comps)
        for d in range(1, reps):
            t = rep_peer(d)
            to_rep(
                g_out.at[turn, t], g_in.at[turn, quarter],
                g_send.at[turn, t], g_recv.at[turn, quarter], t,
            ).start()
        share(phase, y_mine)
        slice_sum = g_out[turn, quarter]
        for d in range(1, reps):
            t = rep_peer(d)
            to_rep(
                g_out.at[turn, t], g_in.at[turn, t],
                g_send.at[turn, t], g_recv.at[turn, t], t,
            ).wait_recv()
            slice_sum = slice_sum + g_in[turn, t]
        slice_out[turn] = slice_sum
        slice_in[turn, me] = slice_sum

        def send_slice(d):
            s = peer(d)
            to_rows(
                slice_out.at[turn], slice_in.at[turn, me],
                slice_send.at[turn, d], slice_recv.at[turn, n - d], s,
            ).start()

        def slice_got(d):
            s = peer(d)
            to_rows(
                slice_out.at[turn], slice_in.at[turn, s],
                slice_send.at[turn, d], slice_recv.at[turn, d], s,
            ).wait_recv()

        over(n, send_slice, 1)
        over(n, slice_got, 1)
        slice_total = jnp.sum(slice_in[turn], axis=0)
        total_out[turn] = slice_total
        for d in range(1, reps):
            t = rep_peer(d)
            to_rep(
                total_out.at[turn], gram.at[turn, quarter],
                total_send.at[turn, t], total_recv.at[turn, quarter], t,
            ).start()
        gram[turn, quarter] = slice_total
        for d in range(1, reps):
            t = rep_peer(d)
            to_rep(
                total_out.at[turn], gram.at[turn, t],
                total_send.at[turn, t], total_recv.at[turn, t], t,
            ).wait_recv()

        inverse_factor(gram.at[turn], elim)
        lower_inv = elim[...]
        shared(phase)
        last = turn == ITERS - 1
        for t in range(reps):
            fresh = dot(y_in[phase, t], lower_inv, ((1,), (1,)), HIGHEST)
            for b in range(blocks):
                low = b * BLOCK + t * piece
                rows = fresh[b * piece:(b + 1) * piece]
                if last:
                    out[low:low + piece] = rows * math.sqrt(slab * n)
                else:
                    u_full[low:low + piece] = (rows * inv[low:low + piece]).astype(BF16)

    def sent_rows(d):
        s = peer(d)
        link_copy(d).wait_send()
        to_rows(picks.at[d], pieces.at[n - d], embed_send.at[d], embed_recv.at[n - d], s).wait_send()
        to_rows(back_out.at[d], back_in.at[n - d], rev_send.at[0, d], rev_recv.at[0, n - d], s).wait_send()
        for phase in range(1, ITERS + 1):
            to_rows(
                rev_out.at[phase, d], rev_in.at[phase, n - d],
                rev_send.at[phase, d], rev_recv.at[phase, n - d], s,
            ).wait_send()
        for turn in range(ITERS):
            to_rows(
                u_out.at[turn, d], u_in.at[turn, n - d],
                u_send.at[turn, d], u_recv.at[turn, n - d], s,
            ).wait_send()
            to_rows(
                slice_out.at[turn], slice_in.at[turn, me],
                slice_send.at[turn, d], slice_recv.at[turn, n - d], s,
            ).wait_send()

    over(n, sent_rows, 1)
    for d in range(1, reps):
        t = rep_peer(d)
        degree_copy(t).wait_send()
        for phase in range(1, ITERS + 1):
            to_rep(
                part_out.at[phase, t], part_in.at[phase, quarter],
                part_send.at[phase, t], part_recv.at[phase, quarter], t,
            ).wait_send()
            to_rep(
                y_own.at[phase], y_in.at[phase, quarter],
                y_send.at[phase, t], y_recv.at[phase, quarter], t,
            ).wait_send()
        for turn in range(ITERS):
            to_rep(
                g_out.at[turn, t], g_in.at[turn, quarter],
                g_send.at[turn, t], g_recv.at[turn, quarter], t,
            ).wait_send()
            to_rep(
                total_out.at[turn], gram.at[turn, quarter],
                total_send.at[turn, t], total_recv.at[turn, quarter], t,
            ).wait_send()


def on_device(n, reps, embed, start, links):
    slab, features = embed.shape
    comps = start.shape[1]
    piece = BLOCK // reps
    own_rows = BLOCKS_DEV * piece
    part = comps // reps
    group = max(1, min(n, LANES // piece))
    phases = ITERS + 1
    vmem = pltpu.VMEM
    sem = pltpu.SemaphoreType.DMA
    scratch = [
        vmem((slab, features), BF16),
        vmem((slab, comps), BF16),
        vmem((8, LANES), jnp.int32),
        vmem((n, 8, LANES), jnp.int32),
        vmem((n, 8, LANES), F32),
        vmem((n, piece, LANES), F32),
        vmem((BLOCKS_DEV, piece, features), BF16),
        vmem((n, piece, features), BF16),
        vmem((n, piece, features), BF16),
        vmem((n // group, group * piece, slab), BF16),
        vmem((n // group, slab, group * piece), BF16),
        vmem((slab, own_rows), BF16),
        vmem((slab, comps), BF16),
        vmem((ITERS, n, piece, comps), BF16),
        vmem((ITERS, n, piece, comps), BF16),
        vmem((phases, n, piece, comps), F32),
        vmem((phases, n, piece, comps), F32),
        vmem((phases, reps, own_rows, comps), F32),
        vmem((phases, reps, own_rows, comps), F32),
        vmem((phases, own_rows, comps), F32),
        vmem((phases, reps, own_rows, comps), F32),
        vmem((slab, comps), F32),
        vmem((own_rows, comps), F32),
        vmem((ITERS, reps, part, comps), F32),
        vmem((ITERS, reps, part, comps), F32),
        vmem((ITERS, part, comps), F32),
        vmem((ITERS, n, part, comps), F32),
        vmem((ITERS, part, comps), F32),
        vmem((ITERS, reps, part, comps), F32),
        vmem((comps, comps), F32),
        vmem((n, 8, LANES), F32),
        vmem((n, 8, LANES), F32),
        vmem((BLOCKS_DEV, 8, LANES), F32),
        vmem((8, slab), F32),
        vmem((reps, 8, slab), F32),
    ]
    sems = [
        (n,), (n,), (n,), (n,), (ITERS, n), (ITERS, n), (phases, n), (phases, n),
        (phases, reps), (phases, reps), (phases, reps), (phases, reps),
        (ITERS, reps), (ITERS, reps), (ITERS, n), (ITERS, n), (ITERS, reps), (ITERS, reps),
        (2,), (reps,), (reps,),
    ]
    return pl.pallas_call(
        functools.partial(kernel, n, reps),
        out_shape=jax.ShapeDtypeStruct((slab, comps), F32),
        in_specs=[pl.BlockSpec(memory_space=pl.ANY)] * 2 + [pl.BlockSpec(memory_space=pltpu.VMEM)],
        out_specs=pl.BlockSpec(memory_space=pltpu.VMEM),
        scratch_shapes=scratch + [sem(shape) for shape in sems],
        compiler_params=pltpu.CompilerParams(
            collective_id=0, has_side_effects=True, vmem_limit_bytes=66 * 1000 * 1000
        ),
        name="spectral",
    )(embed, start, links)


def solution(mesh):
    return jax.shard_map(
        functools.partial(on_device, mesh.shape["rows"], mesh.shape["rep"]),
        mesh=mesh,
        in_specs=(P("rows", None), P("rows", None), P("rows", None)),
        out_specs=P("rows", None),
        check_vma=False,
    )
```

```python
import functools
import math

import jax
import jax.numpy as jnp
from jax import lax
from jax.experimental import pallas as pl
from jax.experimental.pallas import tpu as pltpu
from jax.sharding import PartitionSpec as P

BLOCK = 128
BLOCKS_DEV = 4
ITERS = 2
LANES = 128
PANEL = 16
EPSILON = 1e-06
HIGHEST = lax.Precision.HIGHEST
F32 = jnp.float32
BF16 = jnp.bfloat16


def dot(a, b, dims, precision=None):
    return lax.dot_general(
        a, b, (dims, ((), ())), precision=precision, preferred_element_type=F32
    )


def inv_rms(rows):
    values = rows.astype(F32)
    return lax.rsqrt(jnp.mean(values * values, axis=1, keepdims=True) + EPSILON)


def as_row(column):
    return jnp.broadcast_to(column, (column.shape[0], LANES)).T[0:1, :]


def inverse_factor(matrix, inverse):
    size = matrix.shape[-1]
    count = size // PANEL
    per = matrix.shape[1] // PANEL
    sub = lax.broadcasted_iota(jnp.int32, (PANEL, size), 0)
    lane = lax.broadcasted_iota(jnp.int32, (PANEL, size), 1)
    left = [
        matrix[p // per, (p % per) * PANEL:(p % per + 1) * PANEL, :] for p in range(count)
    ]
    right = [jnp.where(lane == sub + p * PANEL, 1.0, 0.0) for p in range(count)]
    for p in range(count):
        low = p * PANEL
        columns = [
            jnp.broadcast_to(left[p][:, low + j:low + j + 1], (PANEL, size))
            for j in range(PANEL)
        ]
        rows, tracked = left[p], right[p]
        result = jnp.zeros((PANEL, size), F32)
        for k in range(PANEL):
            here = sub == k
            column = columns[k]
            pivot = jnp.broadcast_to(column[k:k + 1, :], (PANEL, size))
            result = jnp.where(here, tracked * lax.rsqrt(pivot), result)
            scale = 1.0 / pivot

            def cleared(values):
                row = values[k:k + 1, :] * scale
                return jnp.where(here, row, values - column * row)

            rows, tracked = cleared(rows), cleared(tracked)
            for j in range(k + 1, PANEL):
                columns[j] = cleared(columns[j])
        for below in range(p + 1, count):
            base = left[below]
            for j in range(PANEL):
                column = base[:, low + j:low + j + 1]
                right[below] = right[below] - column * tracked[j:j + 1, :]
                left[below] = left[below] - column * rows[j:j + 1, :]
        inverse[low:low + PANEL, :] = result


def kernel(
    n, reps,
    embed_hbm, start_hbm, links, out,
    embed, start, link_out, link_in, asked, alive, own, picks, pieces, tiles, tiles_t, square,
    u_full, u_out, u_in, rev_out, rev_in, part_out, part_in, y_own, y_in, inv, placed,
    g_out, g_in, slice_out, slice_in, total_out, gram, elim,
    back_out, back_in, back_sum, degree_out, degree_in,
    link_send, link_recv, embed_send, embed_recv, u_send, u_recv, rev_send, rev_recv,
    part_send, part_recv, y_send, y_recv, g_send, g_recv, slice_send, slice_recv,
    total_send, total_recv, load_sem, degree_send, degree_recv,
):
    me = lax.axis_index("rows")
    quarter = lax.axis_index("rep")
    slab, features = embed.shape
    comps = start.shape[1]
    blocks = BLOCKS_DEV
    piece = BLOCK // reps
    own_rows = blocks * piece
    spread = 2.0 / math.sqrt(features)
    group = max(1, min(n, LANES // piece))
    chunk = group * piece
    unroll = n <= 8

    def over(count, body, low=0):
        if unroll:
            for index in range(low, count):
                body(index)
        else:
            def step(index, carry):
                body(index)
                return carry
            lax.fori_loop(low, count, step, 0)

    def peer(distance):
        return lax.rem(me + distance, n)

    def rep_peer(distance):
        return lax.rem(quarter + distance, reps)

    def to_rows(src, dst, send, recv, target):
        return pltpu.make_async_remote_copy(
            src_ref=src, dst_ref=dst, send_sem=send, recv_sem=recv,
            device_id={"rows": target}, device_id_type=pl.DeviceIdType.MESH,
        )

    def to_rep(src, dst, send, recv, target):
        return pltpu.make_async_remote_copy(
            src_ref=src, dst_ref=dst, send_sem=send, recv_sem=recv,
            device_id={"rep": target}, device_id_type=pl.DeviceIdType.MESH,
        )

    def own_at(block, which):
        return pl.ds(pl.multiple_of(block * BLOCK + which * piece, piece), piece)

    load_embed = pltpu.make_async_copy(embed_hbm, embed, load_sem.at[0])
    load_start = pltpu.make_async_copy(start_hbm, start, load_sem.at[1])
    load_embed.start()
    load_start.start()
    link_out[...] = jnp.full((8, LANES), -1, jnp.int32)
    link_out[0:1, 0:n] = links[...]
    barrier = pltpu.get_barrier_semaphore()

    def greet(distance):
        pl.semaphore_signal(
            barrier, inc=1, device_id={"rows": peer(distance)},
            device_id_type=pl.DeviceIdType.MESH,
        )

    over(n, greet, 1)
    for distance in range(1, reps):
        pl.semaphore_signal(
            barrier, inc=1, device_id={"rep": rep_peer(distance)},
            device_id_type=pl.DeviceIdType.MESH,
        )
    pl.semaphore_wait(barrier, n + reps - 2)

    def link_copy(d):
        return to_rows(link_out, link_in.at[n - d], link_send.at[d], link_recv.at[n - d], peer(d))

    def link_got(d):
        return to_rows(link_out, link_in.at[d], link_send.at[d], link_recv.at[d], peer(d))

    over(n, lambda d: link_copy(d).start(), 1)
    lane = lax.broadcasted_iota(jnp.int32, (8, LANES), 1)
    pieces[0] = jnp.zeros((piece, features), BF16)

    load_embed.wait()
    load_start.wait()
    for b in range(blocks):
        own[b] = embed[own_at(b, quarter), :]
    own_flat = own[...].reshape(own_rows, features)
    own_scale = inv_rms(own_flat)
    slab_scale = jnp.concatenate(
        [inv_rms(embed[b * BLOCK:(b + 1) * BLOCK, :]) for b in range(blocks)], axis=0
    )
    scale_row = as_row(slab_scale)

    def alive_of(d):
        entry = jnp.sum(jnp.where(lane == peer(d), link_out[...], 0).astype(F32), axis=1, keepdims=True)
        alive[d] = jnp.broadcast_to(
            jnp.where(entry[0:1] >= 0.0, 1.0, 0.0), (piece, LANES)
        )

    over(n, alive_of)

    def pick(d):
        s = peer(d)
        link_got(d).wait_recv()
        entry = jnp.sum(
            jnp.where(lane == me, link_in[d], 0).astype(F32), axis=1, keepdims=True
        )
        asked[d] = jnp.broadcast_to(entry, (8, LANES))
        chosen = jnp.maximum(entry[0:1], 0.0)
        mixed = jnp.zeros((piece, features), F32)
        for b in range(blocks):
            mixed = mixed + jnp.where(chosen == float(b), 1.0, 0.0) * own[b].astype(F32)
        picks[d] = mixed.astype(BF16)
        to_rows(picks.at[d], pieces.at[n - d], embed_send.at[d], embed_recv.at[n - d], s).start()

    over(n, pick, 1)

    products = dot(embed[...], own_flat, ((1,), (1,)))
    affinity = jnp.exp(spread * products * slab_scale * as_row(own_scale))
    row_id = lax.broadcasted_iota(jnp.int32, (slab, own_rows), 0)
    col_id = lax.broadcasted_iota(jnp.int32, (slab, own_rows), 1)
    col_row = (col_id // piece) * BLOCK + quarter * piece + col_id % piece
    square[...] = jnp.where(row_id == col_row, 0.0, affinity).astype(BF16)

    def embed_got(d):
        s = peer(d)
        to_rows(picks.at[d], pieces.at[d], embed_send.at[d], embed_recv.at[d], s).wait_recv()


    def tile_chunk(turned):
        index = n // group - 1 - turned
        first = index * group
        if unroll:
            for g in range(group - 1, -1, -1):
                if first + g:
                    embed_got(first + g)
        rows = pieces[pl.ds(first, group)].reshape(chunk, features)
        live = alive[pl.ds(first, group)].reshape(chunk, LANES)[:, 0:1]
        values = dot(rows, embed[...], ((1,), (1,)))
        values = jnp.exp(spread * values * inv_rms(rows) * scale_row) * live
        values = values.astype(BF16)
        tiles[index] = values
        tiles_t[index] = values.astype(F32).T.astype(BF16)

    if not unroll:
        over(n, embed_got, 1)
    over(n // group, tile_chunk)

    def product(phase, u_turn):
        own_us = [u_full[own_at(b, quarter), :] for b in range(blocks)]

        def send_u(d):
            s = peer(d)
            chosen = jnp.maximum(asked[d][0:1, :], 0.0)
            mixed = jnp.zeros((piece, comps), F32)
            for b in range(blocks):
                mixed = mixed + jnp.where(chosen == float(b), 1.0, 0.0) * own_us[b].astype(F32)
            u_out[u_turn, d] = mixed.astype(BF16)
            to_rows(
                u_out.at[u_turn, d], u_in.at[u_turn, n - d],
                u_send.at[u_turn, d], u_recv.at[u_turn, n - d], s,
            ).start()

        over(n, send_u, 1)
        u_in[u_turn, 0] = jnp.zeros((piece, comps), BF16)

        def reverse(index):
            result = dot(tiles[index], u_full[...], ((1,), (0,)))
            rev_out[phase, pl.ds(index * group, group)] = result.astype(BF16).reshape(group, piece, comps)

        over(n // group, reverse)

        def send_rev(d):
            s = peer(d)
            to_rows(
                rev_out.at[phase, d], rev_in.at[phase, n - d],
                rev_send.at[phase, d], rev_recv.at[phase, n - d], s,
            ).start()

        over(n, send_rev, 1)
        u_mine = jnp.concatenate(own_us, axis=0)
        forward = dot(square[...], u_mine, ((1,), (0,)))

        def u_got(d):
            s = peer(d)
            to_rows(
                u_out.at[u_turn, d], u_in.at[u_turn, d],
                u_send.at[u_turn, d], u_recv.at[u_turn, d], s,
            ).wait_recv()

        over(n, u_got, 1)

        def forward_chunk(index, sofar):
            fetched = u_in[u_turn, pl.ds(index * group, group)].reshape(chunk, comps)
            return sofar + dot(tiles_t[index], fetched, ((1,), (0,)))

        if unroll:
            for index in range(n // group):
                forward = forward_chunk(index, forward)
        else:
            forward = lax.fori_loop(0, n // group, forward_chunk, forward)
        for t in range(reps):
            for b in range(blocks):
                low = b * BLOCK + t * piece
                part_out[phase, t, b * piece:(b + 1) * piece] = forward[low:low + piece]
        for d in range(1, reps):
            t = rep_peer(d)
            to_rep(
                part_out.at[phase, t], part_in.at[phase, quarter],
                part_send.at[phase, t], part_recv.at[phase, quarter], t,
            ).start()
        placed[...] = part_out[phase, quarter]

        def place(d):
            s = peer(d)
            to_rows(
                rev_out.at[phase, d], rev_in.at[phase, d],
                rev_send.at[phase, d], rev_recv.at[phase, d], s,
            ).wait_recv()
            chosen = asked[d][0:1, :]
            value = rev_in[phase, d].astype(F32)
            for b in range(blocks):
                at = pl.ds(b * piece, piece)
                placed[at, :] = placed[at, :] + jnp.where(chosen == float(b), 1.0, 0.0) * value

        over(n, place, 1)
        result = placed[...]
        for d in range(1, reps):
            t = rep_peer(d)
            to_rep(
                part_out.at[phase, t], part_in.at[phase, t],
                part_send.at[phase, t], part_recv.at[phase, t], t,
            ).wait_recv()
            result = result + part_in[phase, t]
        return result

    def share(phase, values):
        y_own[phase] = values
        for d in range(1, reps):
            t = rep_peer(d)
            to_rep(
                y_own.at[phase], y_in.at[phase, quarter],
                y_send.at[phase, t], y_recv.at[phase, quarter], t,
            ).start()
        y_in[phase, quarter] = values

    def shared(phase):
        for d in range(1, reps):
            t = rep_peer(d)
            to_rep(
                y_own.at[phase], y_in.at[phase, t],
                y_send.at[phase, t], y_recv.at[phase, t], t,
            ).wait_recv()

    def back_chunk(index):
        sums = dot(jnp.ones((8, slab), BF16), tiles_t[index], ((1,), (0,)))
        for g in range(group):
            back_out[index * group + g, :, 0:piece] = sums[:, g * piece:(g + 1) * piece]

    def send_back(d):
        s = peer(d)
        to_rows(back_out.at[d], back_in.at[n - d], rev_send.at[0, d], rev_recv.at[0, n - d], s).start()

    def back_got(d):
        s = peer(d)
        to_rows(
            back_out.at[d], back_in.at[d], rev_send.at[0, d], rev_recv.at[0, d], s
        ).wait_recv()
        value = back_in[d]
        for b in range(blocks):
            back_sum[b] = back_sum[b] + jnp.where(asked[d] == float(b), 1.0, 0.0) * value

    back_out[...] = jnp.zeros_like(back_out)
    over(n // group, back_chunk)
    over(n, send_back, 1)
    back_sum[...] = jnp.zeros_like(back_sum)
    degree_out[...] = dot(jnp.ones((8, own_rows), BF16), square[...], ((1,), (1,)))

    def own_chunk(index):
        degree_out[...] = degree_out[...] + dot(
            jnp.ones((8, chunk), BF16), tiles[index], ((1,), (0,))
        )

    over(n // group, own_chunk)
    over(n, back_got, 1)
    for b in range(blocks):
        at = pl.ds(b * BLOCK, BLOCK)
        degree_out[:, at] = degree_out[:, at] + pltpu.roll(back_sum[b], quarter * piece, 1)

    def degree_copy(t):
        return to_rep(
            degree_out, degree_in.at[quarter], degree_send.at[t], degree_recv.at[quarter], t
        )

    for d in range(1, reps):
        degree_copy(rep_peer(d)).start()
    degree_in[quarter] = degree_out[...]
    for d in range(1, reps):
        t = rep_peer(d)
        to_rep(
            degree_out, degree_in.at[t], degree_send.at[t], degree_recv.at[t], t
        ).wait_recv()
    inv_row = lax.rsqrt(jnp.sum(degree_in[...], axis=0))[0:1]
    for b in range(blocks):
        inv[b * BLOCK:(b + 1) * BLOCK] = jnp.broadcast_to(
            inv_row[:, b * BLOCK:(b + 1) * BLOCK], (LANES, BLOCK)
        ).T
    inv_own = jnp.concatenate([inv[own_at(b, quarter), 0:comps] for b in range(blocks)], axis=0)
    u_full[...] = (start[...].astype(F32) * inv[...]).astype(BF16)

    part = comps // reps
    for turn in range(ITERS):
        phase = turn + 1
        y_mine = product(phase, turn) * inv_own
        partial = dot(y_mine.T, y_mine, ((1,), (0,)), HIGHEST)
        g_out[turn] = partial.reshape(reps, part, comps)
        for d in range(1, reps):
            t = rep_peer(d)
            to_rep(
                g_out.at[turn, t], g_in.at[turn, quarter],
                g_send.at[turn, t], g_recv.at[turn, quarter], t,
            ).start()
        share(phase, y_mine)
        slice_sum = g_out[turn, quarter]
        for d in range(1, reps):
            t = rep_peer(d)
            to_rep(
                g_out.at[turn, t], g_in.at[turn, t],
                g_send.at[turn, t], g_recv.at[turn, t], t,
            ).wait_recv()
            slice_sum = slice_sum + g_in[turn, t]
        slice_out[turn] = slice_sum
        slice_in[turn, me] = slice_sum

        def send_slice(d):
            s = peer(d)
            to_rows(
                slice_out.at[turn], slice_in.at[turn, me],
                slice_send.at[turn, d], slice_recv.at[turn, n - d], s,
            ).start()

        def slice_got(d):
            s = peer(d)
            to_rows(
                slice_out.at[turn], slice_in.at[turn, s],
                slice_send.at[turn, d], slice_recv.at[turn, d], s,
            ).wait_recv()

        over(n, send_slice, 1)
        over(n, slice_got, 1)
        slice_total = jnp.sum(slice_in[turn], axis=0)
        total_out[turn] = slice_total
        for d in range(1, reps):
            t = rep_peer(d)
            to_rep(
                total_out.at[turn], gram.at[turn, quarter],
                total_send.at[turn, t], total_recv.at[turn, quarter], t,
            ).start()
        gram[turn, quarter] = slice_total
        for d in range(1, reps):
            t = rep_peer(d)
            to_rep(
                total_out.at[turn], gram.at[turn, t],
                total_send.at[turn, t], total_recv.at[turn, t], t,
            ).wait_recv()

        inverse_factor(gram.at[turn], elim)
        lower_inv = elim[...]
        shared(phase)
        last = turn == ITERS - 1
        for t in range(reps):
            fresh = dot(y_in[phase, t], lower_inv, ((1,), (1,)), HIGHEST)
            for b in range(blocks):
                low = b * BLOCK + t * piece
                rows = fresh[b * piece:(b + 1) * piece]
                if last:
                    out[low:low + piece] = rows * math.sqrt(slab * n)
                else:
                    u_full[low:low + piece] = (rows * inv[low:low + piece]).astype(BF16)

    def sent_rows(d):
        s = peer(d)
        link_copy(d).wait_send()
        to_rows(picks.at[d], pieces.at[n - d], embed_send.at[d], embed_recv.at[n - d], s).wait_send()
        to_rows(back_out.at[d], back_in.at[n - d], rev_send.at[0, d], rev_recv.at[0, n - d], s).wait_send()
        for phase in range(1, ITERS + 1):
            to_rows(
                rev_out.at[phase, d], rev_in.at[phase, n - d],
                rev_send.at[phase, d], rev_recv.at[phase, n - d], s,
            ).wait_send()
        for turn in range(ITERS):
            to_rows(
                u_out.at[turn, d], u_in.at[turn, n - d],
                u_send.at[turn, d], u_recv.at[turn, n - d], s,
            ).wait_send()
            to_rows(
                slice_out.at[turn], slice_in.at[turn, me],
                slice_send.at[turn, d], slice_recv.at[turn, n - d], s,
            ).wait_send()

    over(n, sent_rows, 1)
    for d in range(1, reps):
        t = rep_peer(d)
        degree_copy(t).wait_send()
        for phase in range(1, ITERS + 1):
            to_rep(
                part_out.at[phase, t], part_in.at[phase, quarter],
                part_send.at[phase, t], part_recv.at[phase, quarter], t,
            ).wait_send()
            to_rep(
                y_own.at[phase], y_in.at[phase, quarter],
                y_send.at[phase, t], y_recv.at[phase, quarter], t,
            ).wait_send()
        for turn in range(ITERS):
            to_rep(
                g_out.at[turn, t], g_in.at[turn, quarter],
                g_send.at[turn, t], g_recv.at[turn, quarter], t,
            ).wait_send()
            to_rep(
                total_out.at[turn], gram.at[turn, quarter],
                total_send.at[turn, t], total_recv.at[turn, quarter], t,
            ).wait_send()


def on_device(n, reps, embed, start, links):
    slab, features = embed.shape
    comps = start.shape[1]
    piece = BLOCK // reps
    own_rows = BLOCKS_DEV * piece
    part = comps // reps
    group = max(1, min(n, LANES // piece))
    phases = ITERS + 1
    vmem = pltpu.VMEM
    sem = pltpu.SemaphoreType.DMA
    scratch = [
        vmem((slab, features), BF16),
        vmem((slab, comps), BF16),
        vmem((8, LANES), jnp.int32),
        vmem((n, 8, LANES), jnp.int32),
        vmem((n, 8, LANES), F32),
        vmem((n, piece, LANES), F32),
        vmem((BLOCKS_DEV, piece, features), BF16),
        vmem((n, piece, features), BF16),
        vmem((n, piece, features), BF16),
        vmem((n // group, group * piece, slab), BF16),
        vmem((n // group, slab, group * piece), BF16),
        vmem((slab, own_rows), BF16),
        vmem((slab, comps), BF16),
        vmem((ITERS, n, piece, comps), BF16),
        vmem((ITERS, n, piece, comps), BF16),
        vmem((phases, n, piece, comps), BF16),
        vmem((phases, n, piece, comps), BF16),
        vmem((phases, reps, own_rows, comps), F32),
        vmem((phases, reps, own_rows, comps), F32),
        vmem((phases, own_rows, comps), F32),
        vmem((phases, reps, own_rows, comps), F32),
        vmem((slab, comps), F32),
        vmem((own_rows, comps), F32),
        vmem((ITERS, reps, part, comps), F32),
        vmem((ITERS, reps, part, comps), F32),
        vmem((ITERS, part, comps), F32),
        vmem((ITERS, n, part, comps), F32),
        vmem((ITERS, part, comps), F32),
        vmem((ITERS, reps, part, comps), F32),
        vmem((comps, comps), F32),
        vmem((n, 8, LANES), F32),
        vmem((n, 8, LANES), F32),
        vmem((BLOCKS_DEV, 8, LANES), F32),
        vmem((8, slab), F32),
        vmem((reps, 8, slab), F32),
    ]
    sems = [
        (n,), (n,), (n,), (n,), (ITERS, n), (ITERS, n), (phases, n), (phases, n),
        (phases, reps), (phases, reps), (phases, reps), (phases, reps),
        (ITERS, reps), (ITERS, reps), (ITERS, n), (ITERS, n), (ITERS, reps), (ITERS, reps),
        (2,), (reps,), (reps,),
    ]
    return pl.pallas_call(
        functools.partial(kernel, n, reps),
        out_shape=jax.ShapeDtypeStruct((slab, comps), F32),
        in_specs=[pl.BlockSpec(memory_space=pl.ANY)] * 2 + [pl.BlockSpec(memory_space=pltpu.VMEM)],
        out_specs=pl.BlockSpec(memory_space=pltpu.VMEM),
        scratch_shapes=scratch + [sem(shape) for shape in sems],
        compiler_params=pltpu.CompilerParams(
            collective_id=0, has_side_effects=True, vmem_limit_bytes=66 * 1000 * 1000
        ),
        name="spectral",
    )(embed, start, links)


def solution(mesh):
    return jax.shard_map(
        functools.partial(on_device, mesh.shape["rows"], mesh.shape["rep"]),
        mesh=mesh,
        in_specs=(P("rows", None), P("rows", None), P("rows", None)),
        out_specs=P("rows", None),
        check_vma=False,
    )
```
